512 devices in a mesh: section: 16 (over x, z_hi), rep: 32 (over z_lo, y, core).
Axes of the slice: x: 4, y: 8, z: 8 (z_hi: 4, z_lo: 2; z = z_hi * 2 + z_lo), core: 2. Of those that a mesh axis runs over, the one named last changes fastest.
Arguments:
- features: bfloat16 [131072, 128], P(('section', 'rep')), may hold values from -6 to 6
- inv_degree: float32 [131072], P(('section', 'rep')), may hold values from 0.03 to 0.3
- weight: bfloat16 [128, 128], replicated, may hold values from -0.5 to 0.5
- bias_vector: float32 [128], replicated, may hold values from -3 to 3
- tile_values: bfloat16 [512, 16, 8, 128, 128], P(('section', 'rep')), may hold values from 0 to 1
- tile_rows: int32 [512, 16, 8], P(('section', 'rep')), may hold values from 0 to 63, as said below
- tile_cols: int32 [512, 16, 8], P(('section', 'rep')), may hold values from 0 to 1
- tile_counts: int32 [512, 16], P(('section', 'rep')), may hold values from 0 to 8, as said below
Outputs:
- output: bfloat16 [131072, 128], P(('section', 'rep'))
The draws below stay inside these ranges and needn't reach their ends.
Inputs may be any that keep to these rules, and one draw needn't show every extreme that they name: `tile_rows`: within one device and column section no pair of tile row and tile column repeats among the slots. `tile_counts`: slots beyond the count are not read. In every draw some device has 8 live slots for some column section.
All inputs are finite; a program needn't handle non-finite values.
Results may differ from the reference program's by a relative error of at most 0.023.
Values may be sent and summed in bfloat16 or wider, within the bound.
A program may use at most 64 MiB of HBM per device.

```python
import math
import jax
import jax.numpy as jnp
from jax import lax

F = 128
H = 128
TILE = 128
RB = 2
CAPS = 8
NODES = 131072
N_SECTION = 16
N_REP = 32


def tile_slots(key):
    groups = N_SECTION * N_REP * N_SECTION
    candidates = N_REP * RB * RB
    scores = jax.random.randint(jax.random.fold_in(key, 7), (groups, candidates), 0, 1 << 20) * candidates
    scores = scores + jnp.arange(candidates, dtype=jnp.int32)[None, :]
    chosen = jnp.argsort(scores, axis=1)[:, :CAPS].astype(jnp.int32)
    return chosen.reshape(N_SECTION * N_REP, N_SECTION, CAPS)


def draw_tile_rows(key, part):
    return tile_slots(key) // RB


def draw_tile_cols(key, part):
    return tile_slots(key) % RB


def draw_tile_counts(key, part):
    devices = N_SECTION * N_REP
    first_key, second_key, third_key, fourth_key = jax.random.split(jax.random.fold_in(key, 11), 4)
    level = jax.random.randint(first_key, (devices,), 1, CAPS + 1)
    picked = jax.random.randint(second_key, (), 0, devices)
    device_ids = jnp.arange(devices, dtype=jnp.int32)
    level = jnp.where(device_ids == picked, CAPS, level)
    lowest = level // 2
    counts = jax.random.randint(third_key, (devices, N_SECTION), lowest[:, None], level[:, None] + 1)
    section_pick = jax.random.randint(fourth_key, (), 0, N_SECTION)
    section_ids = jnp.arange(N_SECTION, dtype=jnp.int32)
    full_slot = (device_ids[:, None] == picked) & (section_ids[None, :] == section_pick)
    return jnp.where(full_slot, CAPS, counts).astype(jnp.int32)


def levels(stream_key, shape, cuts, smallest, high):
    loudness = 1.0
    for axis_at, parts in cuts:
        heights = jax.random.uniform(jax.random.fold_in(jax.random.fold_in(stream_key, 6), axis_at), (parts,), jnp.float32, smallest / len(cuts), high / len(cuts))
        loudness = loudness * jnp.repeat(jnp.exp(heights), shape[axis_at] // parts).reshape((-1,) + (1,) * (len(shape) - 1 - axis_at))
    return loudness


def noise(rng, dims, deviation, bound, cuts=(), kind=jnp.bfloat16):
    values = deviation * jax.random.normal(rng, dims, jnp.float32)
    if cuts:
        values = values * levels(rng, dims, cuts, -0.22, 0.18)
    return jnp.clip(values, -bound, bound).astype(kind)


def setup_inputs(seed: int = 0) -> dict:
    seeds = jax.random.split(jax.random.key(seed), 9)
    return {
        "features": noise(seeds[0], (NODES, F), 1.0, 6.0, ((0, 512),)),
        "inv_degree": jnp.clip(jnp.exp(math.log(0.3) - 2.3025852 * jax.random.uniform(seeds[1], (NODES,), jnp.float32) ** levels(seeds[1], (NODES,), ((0, 512),), -0.2, 0.2)), 0.03, 0.3),
        "weight": noise(seeds[2], (F, H), F ** -0.5, 0.5),
        "bias_vector": noise(seeds[3], (H,), 0.5, 3.0, (), jnp.float32),
        "tile_values": jnp.clip(1.0 * jax.random.uniform(seeds[4], (N_SECTION * N_REP, N_SECTION, CAPS, TILE, TILE), jnp.float32) ** levels(seeds[4], (N_SECTION * N_REP, N_SECTION, CAPS, TILE, TILE), ((0, 512),), -0.2, 0.2), 0.0, 1.0).astype(jnp.bfloat16),
        "tile_rows": draw_tile_rows(jax.random.fold_in(seeds[8], 71), 0),
        "tile_cols": draw_tile_cols(jax.random.fold_in(seeds[8], 71), 0),
        "tile_counts": draw_tile_counts(jax.random.fold_in(seeds[8], 71), 0),
    }


def reference(features, inv_degree, weight, bias_vector, tile_values, tile_rows, tile_cols, tile_counts):
    scaled = (inv_degree[:, None] * features.astype(jnp.float32)).astype(jnp.bfloat16)
    pieces = scaled.reshape(N_SECTION, N_REP, RB, TILE, F)
    section_ids = jnp.arange(N_SECTION, dtype=jnp.int32)[:, None]
    slot_ids = jnp.arange(CAPS, dtype=jnp.int32)[None, :]
    block_rows = N_REP * RB * TILE

    def per_device(aggregate, device_index):
        section_index = device_index // N_REP
        rep_index = device_index % N_REP
        column_pieces = lax.dynamic_index_in_dim(pieces, rep_index, 1, keepdims=False)
        sources = column_pieces[section_ids, tile_cols[device_index]].astype(jnp.float32)
        values = tile_values[device_index].astype(jnp.float32)
        products = jnp.einsum("tkij,tkjf->tkif", values, sources)
        alive_mask = slot_ids < tile_counts[device_index][:, None]
        products = jnp.where(alive_mask[:, :, None, None], products, 0.0)
        block_sum = jnp.zeros((N_REP * RB, TILE, F), jnp.float32)
        block_sum = block_sum.at[tile_rows[device_index].reshape(-1)].add(products.reshape(N_SECTION * CAPS, TILE, F))
        row_start = (section_index * block_rows).astype(jnp.int32)
        current = lax.dynamic_slice_in_dim(aggregate, row_start, block_rows, 0)
        aggregate = lax.dynamic_update_slice_in_dim(aggregate, current + block_sum.reshape(block_rows, F), row_start, 0)
        return aggregate, None

    aggregate, _ = lax.scan(per_device, jnp.zeros((NODES, F), jnp.float32), jnp.arange(N_SECTION * N_REP, dtype=jnp.int32))
    normed = (inv_degree[:, None] * aggregate).astype(jnp.bfloat16)
    hidden = jnp.dot(normed, weight, preferred_element_type=jnp.float32) + bias_vector
    return jnp.maximum(hidden, 0.0).astype(jnp.bfloat16)
```

```python
import jax
import jax.numpy as jnp
from jax import lax
from jax.experimental import pallas as pl
from jax.experimental.pallas import tpu as pltpu
from jax.sharding import PartitionSpec as P

MESH = pl.DeviceIdType.MESH
VMEM_LIMIT = 60 * 1024 * 1024


def meet(axis, peers):
    barrier = pltpu.get_barrier_semaphore()
    for peer in peers:
        pl.semaphore_signal(barrier, inc=1, device_id={axis: peer}, device_id_type=MESH)
    pl.semaphore_wait(barrier, len(peers))


def gather_kernel(own_ref, out_ref, send_sems, recv_sems, local_sem):
    me = lax.axis_index("section")
    x, z = me // 4, me % 4
    half = own_ref.shape[0] // 2

    def sec(dx, dz):
        return ((x + dx) % 4) * 4 + (z + dz) % 4

    zp, zm, xp, xm = sec(0, 1), sec(0, 3), sec(1, 0), sec(3, 0)
    meet("section", (zp, zm, xp, xm))
    sends = []

    def send(slot, h, peer, own=False):
        rows = pl.ds(h * half, half)
        copy = pltpu.make_async_remote_copy(
            src_ref=own_ref.at[rows] if own else out_ref.at[slot, rows],
            dst_ref=out_ref.at[slot, rows],
            send_sem=send_sems.at[len(sends)],
            recv_sem=recv_sems.at[slot, h],
            device_id={"section": peer},
            device_id_type=MESH,
        )
        copy.start()
        sends.append(copy)

    waited = set()

    def need(dx, dz, h):
        if (dx, dz, h) in waited:
            return
        waited.add((dx, dz, h))
        slot, rows = sec(dx, dz), pl.ds(h * half, half)
        pltpu.make_async_remote_copy(
            src_ref=out_ref.at[slot, rows],
            dst_ref=out_ref.at[slot, rows],
            send_sem=send_sems.at[0],
            recv_sem=recv_sems.at[slot, h],
            device_id={"section": zp},
            device_id_type=MESH,
        ).wait_recv()

    for h, peer in ((0, zp), (1, zm), (1, zp), (0, zm), (0, xp), (1, xm), (1, xp), (0, xm)):
        send(me, h, peer, own=True)
    keep = pltpu.make_async_copy(own_ref, out_ref.at[me], local_sem)
    keep.start()

    need(0, 3, 0)
    send(sec(0, 3), 0, zp)
    need(0, 1, 1)
    send(sec(0, 1), 1, zm)
    send(sec(0, 3), 0, xp)
    send(sec(0, 1), 1, xm)
    need(3, 0, 0)
    send(sec(3, 0), 0, xp)
    need(1, 0, 1)
    send(sec(1, 0), 1, xm)
    send(sec(0, 1), 1, xp)
    send(sec(0, 3), 0, xm)
    need(0, 3, 1)
    send(sec(0, 3), 1, xp)
    send(sec(0, 3), 1, xm)
    need(0, 1, 0)
    send(sec(0, 1), 0, xp)
    send(sec(0, 1), 0, xm)
    need(3, 3, 0)
    send(sec(3, 3), 0, xp)
    need(1, 1, 1)
    send(sec(1, 1), 1, xm)
    need(0, 2, 0)
    send(sec(0, 2), 0, xp)
    send(sec(0, 2), 0, xm)
    need(0, 2, 1)
    send(sec(0, 2), 1, xm)
    send(sec(0, 2), 1, xp)
    need(1, 3, 1)
    send(sec(1, 3), 1, xm)
    need(3, 1, 0)
    send(sec(3, 1), 0, xp)
    need(3, 2, 0)
    send(sec(3, 2), 0, xp)
    need(1, 2, 1)
    send(sec(1, 2), 1, xm)
    for dx in range(4):
        for dz in range(4):
            for h in range(2):
                if (dx, dz) != (0, 0):
                    need(dx, dz, h)
    keep.wait()
    for copy in sends:
        copy.wait_send()


def tiles_kernel(
    rows_ref, cols_ref, counts_ref, pieces_ref, values_ref, out_ref, held, total, sems
):
    sections, caps = rows_ref.shape
    tile = total.shape[1]
    tile_rows = total.shape[0] - 1
    loads = []
    for t in range(sections):
        loads.append(pltpu.make_async_copy(values_ref.at[t], held.at[t], sems.at[t]))
        loads[-1].start()
    total[...] = jnp.zeros_like(total)

    def body(t, carry):
        pltpu.make_async_copy(values_ref.at[t], held.at[t], sems.at[t]).wait()
        right = jnp.concatenate([pieces_ref[t, 0:tile, :], pieces_ref[t, tile : 2 * tile, :]], axis=1)
        left = held[t].reshape(caps * tile, tile)
        both = jnp.dot(left, right, preferred_element_type=jnp.float32)
        for k in range(caps):
            row = jnp.where(k < counts_ref[t], rows_ref[t, k], tile_rows)
            part = both[k * tile : (k + 1) * tile, :]
            total[row] += jnp.where(cols_ref[t, k] == 0, part[:, :tile], part[:, tile:])
        return carry

    lax.fori_loop(0, sections, body, 0)
    for core in range(2):
        for y in range(8):
            for z in range(2):
                for h in range(2):
                    out_ref[core, y, z, h] = total[((z * 8 + y) * 2 + core) * 2 + h].astype(
                        out_ref.dtype
                    )


def scatter_kernel(
    part_ref, out_ref, mate, first, runs, zout, zin,
    mate_send, mate_recv, run_send, run_recv, z_send, z_recv,
):
    me = lax.axis_index("rep")
    core, y, z = me % 2, (me // 2) % 8, me // 16
    tile = out_ref.shape[0] // 2

    def rep(zz, yy, cc):
        return (zz * 8 + yy % 8) * 2 + cc

    other = rep(z, y, 1 - core)
    steps = (rep(z, y + 1, core), rep(z, y + 7, core))
    across = rep(1 - z, y, core)
    meet("rep", (other, steps[0], steps[1], across))

    swaps = {}
    for dy in (4, 3, 5, 2, 6, 1, 7, 0):
        at = (y + dy) % 8
        swaps[dy] = pltpu.make_async_remote_copy(
            src_ref=part_ref.at[1 - core, at],
            dst_ref=mate.at[at],
            send_sem=mate_send.at[dy],
            recv_sem=mate_recv.at[dy],
            device_id={"rep": other},
            device_id_type=MESH,
        )
        swaps[dy].start()
    swapped = set()

    def term(dy, zi, h):
        dy = dy % 8
        if dy not in swapped:
            swapped.add(dy)
            swaps[dy].wait_recv()
        at = (y + dy) % 8
        zz = 1 - z if zi == 0 else z
        return part_ref[core, at, zz, h].astype(jnp.float32) + mate[at, zz, h].astype(jnp.float32)

    def hops(d, h):
        return 4 if d != h else 3

    copies = {}
    for s in range(4):
        for zi in range(2):
            for d, h in ((0, 1), (1, 0), (0, 0), (1, 1)):
                length = hops(d, h)
                if s >= length:
                    continue
                dy = (length - s) * (1 - 2 * d)
                value = term(dy, zi, h)
                if s == 0:
                    buf = first.at[d, h, zi]
                else:
                    copies[d, h, zi, s - 1].wait_recv()
                    buf = runs.at[d, h, zi, s - 1]
                    value = value + buf[...].astype(jnp.float32)
                buf[...] = value.astype(jnp.bfloat16)
                copies[d, h, zi, s] = pltpu.make_async_remote_copy(
                    src_ref=buf,
                    dst_ref=runs.at[d, h, zi, s],
                    send_sem=run_send.at[d, h, zi, s],
                    recv_sem=run_recv.at[d, h, zi, s],
                    device_id={"rep": steps[d]},
                    device_id_type=MESH,
                )
                copies[d, h, zi, s].start()

    def gathered(zi, h):
        value = term(0, zi, h)
        for d in range(2):
            last = hops(d, h) - 1
            copies[d, h, zi, last].wait_recv()
            value = value + runs[d, h, zi, last].astype(jnp.float32)
        return value

    crosses = []
    for h in range(2):
        zout[h] = gathered(0, h).astype(jnp.bfloat16)
        crosses.append(
            pltpu.make_async_remote_copy(
                src_ref=zout.at[h],
                dst_ref=zin.at[h],
                send_sem=z_send.at[h],
                recv_sem=z_recv.at[h],
                device_id={"rep": across},
                device_id_type=MESH,
            )
        )
        crosses[h].start()
    mine = [gathered(1, h) for h in range(2)]
    for h in range(2):
        crosses[h].wait_recv()
        out_ref[h * tile : (h + 1) * tile, :] = mine[h] + zin[h].astype(jnp.float32)
    for copy in list(swaps.values()) + list(copies.values()) + crosses:
        copy.wait_send()


def shards(
    features, inv_degree, weight, bias_vector, tile_values, tile_rows, tile_cols, tile_counts
):
    rows_dev, width = features.shape
    sections, caps, tile = tile_values.shape[1:4]
    vmem = pl.BlockSpec(memory_space=pltpu.VMEM)
    smem = pl.BlockSpec(memory_space=pltpu.SMEM)
    bf16, f32 = jnp.bfloat16, jnp.float32
    dma = pltpu.SemaphoreType.DMA
    scaled = (inv_degree[:, None] * features.astype(f32)).astype(bf16)
    pieces = pl.pallas_call(
        gather_kernel,
        out_shape=jax.ShapeDtypeStruct((16, rows_dev, width), bf16),
        in_specs=[vmem],
        out_specs=vmem,
        scratch_shapes=[dma((30,)), dma((16, 2)), dma],
        compiler_params=pltpu.CompilerParams(
            collective_id=0, has_side_effects=True, vmem_limit_bytes=VMEM_LIMIT
        ),
        name="gather_pieces",
    )(scaled)
    partial = pl.pallas_call(
        tiles_kernel,
        out_shape=jax.ShapeDtypeStruct((2, 8, 2, 2, tile, width), bf16),
        in_specs=[smem, smem, smem, vmem, pl.BlockSpec(memory_space=pl.ANY)],
        out_specs=vmem,
        scratch_shapes=[
            pltpu.VMEM((sections, caps, tile, tile), bf16),
            pltpu.VMEM((65, tile, width), f32),
            dma((sections,)),
        ],
        compiler_params=pltpu.CompilerParams(vmem_limit_bytes=VMEM_LIMIT),
        name="tile_products",
    )(tile_rows[0], tile_cols[0], tile_counts[0], pieces, tile_values[0])
    summed = pl.pallas_call(
        scatter_kernel,
        out_shape=jax.ShapeDtypeStruct((rows_dev, width), f32),
        in_specs=[vmem],
        out_specs=vmem,
        scratch_shapes=[
            pltpu.VMEM((8, 2, 2, tile, width), bf16),
            pltpu.VMEM((2, 2, 2, tile, width), bf16),
            pltpu.VMEM((2, 2, 2, 4, tile, width), bf16),
            pltpu.VMEM((2, tile, width), bf16),
            pltpu.VMEM((2, tile, width), bf16),
            dma((8,)),
            dma((8,)),
            dma((2, 2, 2, 4)),
            dma((2, 2, 2, 4)),
            dma((2,)),
            dma((2,)),
        ],
        compiler_params=pltpu.CompilerParams(
            collective_id=1, has_side_effects=True, vmem_limit_bytes=VMEM_LIMIT
        ),
        name="scatter_sums",
    )(partial)
    normed = (inv_degree[:, None] * summed).astype(bf16)
    hidden = jnp.dot(normed, weight, preferred_element_type=f32) + bias_vector
    return jnp.maximum(hidden, 0.0).astype(bf16)


def solution(mesh):
    return jax.shard_map(
        shards,
        mesh=mesh,
        in_specs=(
            P(("section", "rep"), None),
            P(("section", "rep")),
            P(),
            P(),
            P(("section", "rep"), None, None, None, None),
            P(("section", "rep"), None, None),
            P(("section", "rep"), None, None),
            P(("section", "rep"), None),
        ),
        out_specs=P(("section", "rep"), None),
        check_vma=False,
    )
```

```python
import jax
import jax.numpy as jnp
from jax import lax
from jax.experimental import pallas as pl
from jax.experimental.pallas import tpu as pltpu
from jax.sharding import PartitionSpec as P

MESH = pl.DeviceIdType.MESH
MIB = 1024 * 1024


def greet(axis, peers):
    barrier = pltpu.get_barrier_semaphore()
    for peer in peers:
        pl.semaphore_signal(barrier, inc=1, device_id={axis: peer}, device_id_type=MESH)
    return lambda: pl.semaphore_wait(barrier, len(peers))


def gather_kernel(
    features_hbm, inv_hbm, values_hbm, out_ref, values_ref,
    features_ref, inv_ref, send_sems, recv_sems, load_sems, value_sems,
):
    me = lax.axis_index("section")
    x, z = me // 4, me % 4
    half = features_ref.shape[0] // 2

    def sec(dx, dz):
        return ((x + dx) % 4) * 4 + (z + dz) % 4

    zp, zm, xp, xm = sec(0, 1), sec(0, 3), sec(1, 0), sec(3, 0)
    met = greet("section", (zp, zm, xp, xm))
    loads = [
        pltpu.make_async_copy(features_hbm, features_ref, load_sems.at[0]),
        pltpu.make_async_copy(inv_hbm, inv_ref, load_sems.at[1]),
    ]
    for load in loads:
        load.start()
    fills = [
        pltpu.make_async_copy(values_hbm.at[t], values_ref.at[t], value_sems.at[t])
        for t in range(values_ref.shape[0])
    ]
    for load in loads:
        load.wait()
    for fill in fills:
        fill.start()
    for h in range(2):
        rows = slice(h * half, (h + 1) * half)
        column = jnp.transpose(jnp.broadcast_to(inv_ref[h : h + 1, :], (half, half)))
        scaled = column * features_ref[rows, :].astype(jnp.float32)
        out_ref[me, rows, :] = scaled.astype(out_ref.dtype)
    met()
    sends = []

    def send(slot, h, peer):
        rows = pl.ds(h * half, half)
        copy = pltpu.make_async_remote_copy(
            src_ref=out_ref.at[slot, rows],
            dst_ref=out_ref.at[slot, rows],
            send_sem=send_sems.at[len(sends)],
            recv_sem=recv_sems.at[slot, h],
            device_id={"section": peer},
            device_id_type=MESH,
        )
        copy.start()
        sends.append(copy)

    waited = set()

    def need(dx, dz, h):
        if (dx, dz, h) in waited:
            return
        waited.add((dx, dz, h))
        slot, rows = sec(dx, dz), pl.ds(h * half, half)
        pltpu.make_async_remote_copy(
            src_ref=out_ref.at[slot, rows],
            dst_ref=out_ref.at[slot, rows],
            send_sem=send_sems.at[0],
            recv_sem=recv_sems.at[slot, h],
            device_id={"section": zp},
            device_id_type=MESH,
        ).wait_recv()

    for h, peer in ((0, zp), (1, zm), (1, zp), (0, zm), (0, xp), (1, xm), (1, xp), (0, xm)):
        send(me, h, peer)

    need(0, 3, 0)
    send(sec(0, 3), 0, zp)
    need(0, 1, 1)
    send(sec(0, 1), 1, zm)
    send(sec(0, 3), 0, xp)
    send(sec(0, 1), 1, xm)
    need(3, 0, 0)
    send(sec(3, 0), 0, xp)
    need(1, 0, 1)
    send(sec(1, 0), 1, xm)
    send(sec(0, 1), 1, xp)
    send(sec(0, 3), 0, xm)
    need(0, 3, 1)
    send(sec(0, 3), 1, xp)
    send(sec(0, 3), 1, xm)
    need(0, 1, 0)
    send(sec(0, 1), 0, xp)
    send(sec(0, 1), 0, xm)
    need(3, 3, 0)
    send(sec(3, 3), 0, xp)
    need(1, 1, 1)
    send(sec(1, 1), 1, xm)
    need(0, 2, 0)
    send(sec(0, 2), 0, xp)
    send(sec(0, 2), 0, xm)
    need(0, 2, 1)
    send(sec(0, 2), 1, xm)
    send(sec(0, 2), 1, xp)
    need(1, 3, 1)
    send(sec(1, 3), 1, xm)
    need(3, 1, 0)
    send(sec(3, 1), 0, xp)
    need(3, 2, 0)
    send(sec(3, 2), 0, xp)
    need(1, 2, 1)
    send(sec(1, 2), 1, xm)
    for dx in range(4):
        for dz in range(4):
            for h in range(2):
                if (dx, dz) != (0, 0):
                    need(dx, dz, h)
    for fill in fills:
        fill.wait()
    for copy in sends:
        copy.wait_send()


def tiles_kernel(
    rows_hbm, cols_hbm, counts_hbm, pieces_ref, values_ref, out_ref,
    rows_ref, cols_ref, counts_ref, total, sems,
):
    loads = [
        pltpu.make_async_copy(source, target, sems.at[i])
        for i, (source, target) in enumerate(
            ((rows_hbm, rows_ref), (cols_hbm, cols_ref), (counts_hbm, counts_ref))
        )
    ]
    for load in loads:
        load.start()
    caps, sections = rows_ref.shape
    tile = total.shape[1]
    tile_rows = total.shape[0] - 1
    total[...] = jnp.zeros_like(total)
    for load in loads:
        load.wait()

    def body(t, carry):
        right = jnp.concatenate([pieces_ref[t, 0:tile, :], pieces_ref[t, tile : 2 * tile, :]], axis=1)
        left = values_ref[t].reshape(caps * tile, tile)
        both = jnp.dot(left, right, preferred_element_type=jnp.float32)
        for k in range(caps):
            row = jnp.where(k < counts_ref[0, t], rows_ref[k, t], tile_rows)
            part = both[k * tile : (k + 1) * tile, :]
            total[row] += jnp.where(cols_ref[k, t] == 0, part[:, :tile], part[:, tile:])
        return carry

    lax.fori_loop(0, sections, body, 0)
    for core in range(2):
        for y in range(8):
            for z in range(2):
                for h in range(2):
                    out_ref[core, y, z, h] = total[((z * 8 + y) * 2 + core) * 2 + h].astype(
                        out_ref.dtype
                    )


def scatter_kernel(
    part_ref, out_ref, mate, first, runs, zout, zin,
    mate_send, mate_recv, run_send, run_recv, z_send, z_recv,
):
    me = lax.axis_index("rep")
    core, y, z = me % 2, (me // 2) % 8, me // 16
    tile = out_ref.shape[0] // 2

    def rep(zz, yy, cc):
        return (zz * 8 + yy % 8) * 2 + cc

    other = rep(z, y, 1 - core)
    steps = (rep(z, y + 1, core), rep(z, y + 7, core))
    across = rep(1 - z, y, core)
    greet("rep", (other, steps[0], steps[1], across))()

    swaps = {}
    for dy in (4, 3, 5, 2, 6, 1, 7, 0):
        at = (y + dy) % 8
        swaps[dy] = pltpu.make_async_remote_copy(
            src_ref=part_ref.at[1 - core, at],
            dst_ref=mate.at[at],
            send_sem=mate_send.at[dy],
            recv_sem=mate_recv.at[dy],
            device_id={"rep": other},
            device_id_type=MESH,
        )
        swaps[dy].start()
    swapped = set()

    def term(dy, zi, h):
        dy = dy % 8
        if dy not in swapped:
            swapped.add(dy)
            swaps[dy].wait_recv()
        at = (y + dy) % 8
        zz = 1 - z if zi == 0 else z
        return part_ref[core, at, zz, h].astype(jnp.float32) + mate[at, zz, h].astype(jnp.float32)

    def hops(d, h):
        return 4 if d != h else 3

    copies = {}
    for s in range(4):
        for zi in range(2):
            for d, h in ((0, 1), (1, 0), (0, 0), (1, 1)):
                length = hops(d, h)
                if s >= length:
                    continue
                dy = (length - s) * (1 - 2 * d)
                value = term(dy, zi, h)
                if s == 0:
                    buf = first.at[d, h, zi]
                else:
                    copies[d, h, zi, s - 1].wait_recv()
                    buf = runs.at[d, h, zi, s - 1]
                    value = value + buf[...].astype(jnp.float32)
                buf[...] = value.astype(jnp.bfloat16)
                copies[d, h, zi, s] = pltpu.make_async_remote_copy(
                    src_ref=buf,
                    dst_ref=runs.at[d, h, zi, s],
                    send_sem=run_send.at[d, h, zi, s],
                    recv_sem=run_recv.at[d, h, zi, s],
                    device_id={"rep": steps[d]},
                    device_id_type=MESH,
                )
                copies[d, h, zi, s].start()

    def gathered(zi, h):
        value = term(0, zi, h)
        for d in range(2):
            last = hops(d, h) - 1
            copies[d, h, zi, last].wait_recv()
            value = value + runs[d, h, zi, last].astype(jnp.float32)
        return value

    crosses = []
    for h in range(2):
        zout[h] = gathered(0, h).astype(jnp.bfloat16)
        crosses.append(
            pltpu.make_async_remote_copy(
                src_ref=zout.at[h],
                dst_ref=zin.at[h],
                send_sem=z_send.at[h],
                recv_sem=z_recv.at[h],
                device_id={"rep": across},
                device_id_type=MESH,
            )
        )
        crosses[h].start()
    mine = [gathered(1, h) for h in range(2)]
    for h in range(2):
        crosses[h].wait_recv()
        out_ref[h * tile : (h + 1) * tile, :] = mine[h] + zin[h].astype(jnp.float32)
    for copy in list(swaps.values()) + list(copies.values()) + crosses:
        copy.wait_send()


def shards(
    features, inv_degree, weight, bias_vector, tile_values, tile_rows, tile_cols, tile_counts
):
    rows_dev, width = features.shape
    sections, caps, tile = tile_values.shape[1:4]
    vmem = pl.BlockSpec(memory_space=pltpu.VMEM)
    hbm = pl.BlockSpec(memory_space=pltpu.HBM)
    bf16, f32 = jnp.bfloat16, jnp.float32
    dma = pltpu.SemaphoreType.DMA
    pieces, values = pl.pallas_call(
        gather_kernel,
        out_shape=(
            pltpu.VMEM((16, rows_dev, width), bf16),
            pltpu.VMEM(tile_values.shape[1:], bf16),
        ),
        in_specs=[hbm, hbm, hbm],
        out_specs=(vmem, vmem),
        scratch_shapes=[
            pltpu.VMEM((rows_dev, width), bf16),
            pltpu.VMEM((2, rows_dev // 2), f32),
            dma((30,)),
            dma((16, 2)),
            dma((2,)),
            dma((sections,)),
        ],
        compiler_params=pltpu.CompilerParams(
            collective_id=0, has_side_effects=True, vmem_limit_bytes=57 * MIB
        ),
        cost_estimate=pl.CostEstimate(flops=0, bytes_accessed=48 * MIB, transcendentals=0),
        name="gather_pieces",
    )(features, inv_degree.reshape(2, rows_dev // 2), tile_values[0])
    partial = pl.pallas_call(
        tiles_kernel,
        out_shape=jax.ShapeDtypeStruct((2, 8, 2, 2, tile, width), bf16),
        in_specs=[hbm, hbm, hbm, vmem, vmem],
        out_specs=vmem,
        scratch_shapes=[
            pltpu.SMEM((caps, sections), jnp.int32),
            pltpu.SMEM((caps, sections), jnp.int32),
            pltpu.SMEM((1, sections), jnp.int32),
            pltpu.VMEM((65, tile, width), f32),
            dma((3,)),
        ],
        compiler_params=pltpu.CompilerParams(vmem_limit_bytes=20 * MIB),
        name="tile_products",
    )(tile_rows[0].T, tile_cols[0].T, tile_counts, pieces, values)
    summed = pl.pallas_call(
        scatter_kernel,
        out_shape=jax.ShapeDtypeStruct((rows_dev, width), f32),
        in_specs=[vmem],
        out_specs=vmem,
        scratch_shapes=[
            pltpu.VMEM((8, 2, 2, tile, width), bf16),
            pltpu.VMEM((2, 2, 2, tile, width), bf16),
            pltpu.VMEM((2, 2, 2, 4, tile, width), bf16),
            pltpu.VMEM((2, tile, width), bf16),
            pltpu.VMEM((2, tile, width), bf16),
            dma((8,)),
            dma((8,)),
            dma((2, 2, 2, 4)),
            dma((2, 2, 2, 4)),
            dma((2,)),
            dma((2,)),
        ],
        compiler_params=pltpu.CompilerParams(
            collective_id=1, has_side_effects=True, vmem_limit_bytes=16 * MIB
        ),
        cost_estimate=pl.CostEstimate(flops=0, bytes_accessed=48 * MIB, transcendentals=0),
        name="scatter_sums",
    )(partial)
    normed = (inv_degree[:, None] * summed).astype(bf16)
    hidden = jnp.dot(normed, weight, preferred_element_type=f32) + bias_vector
    return jnp.maximum(hidden, 0.0).astype(bf16)


def solution(mesh):
    return jax.shard_map(
        shards,
        mesh=mesh,
        in_specs=(
            P(("section", "rep"), None),
            P(("section", "rep")),
            P(),
            P(),
            P(("section", "rep"), None, None, None, None),
            P(("section", "rep"), None, None),
            P(("section", "rep"), None, None),
            P(("section", "rep"), None),
        ),
        out_specs=P(("section", "rep"), None),
        check_vma=False,
    )
```

```python
import jax
import jax.numpy as jnp
from jax import lax
from jax.experimental import pallas as pl
from jax.experimental.pallas import tpu as pltpu
from jax.sharding import PartitionSpec as P

MESH = pl.DeviceIdType.MESH
MIB = 1024 * 1024
PARTS = ((0, 96, "zx", 0), (96, 96, "zx", 1), (192, 32, "xz", 0), (224, 32, "xz", 1))


def greet(axis, peers):
    barrier = pltpu.get_barrier_semaphore()
    for peer in peers:
        pl.semaphore_signal(barrier, inc=1, device_id={axis: peer}, device_id_type=MESH)
    return lambda: pl.semaphore_wait(barrier, len(peers))


def gather_kernel(
    features_hbm, inv_hbm, values_hbm, out_ref, values_ref,
    features_ref, inv_ref, send_sems, recv_sems, load_sems, value_sems,
):
    me = lax.axis_index("section")
    x, z = me // 4, me % 4
    half = features_ref.shape[0] // 2

    def sec(dx, dz):
        return ((x + dx) % 4) * 4 + (z + dz) % 4

    zp, zm, xp, xm = sec(0, 1), sec(0, 3), sec(1, 0), sec(3, 0)
    met = greet("section", (zp, zm, xp, xm))
    loads = [
        pltpu.make_async_copy(features_hbm, features_ref, load_sems.at[0]),
        pltpu.make_async_copy(inv_hbm, inv_ref, load_sems.at[1]),
    ]
    for load in loads:
        load.start()
    fills = [
        pltpu.make_async_copy(values_hbm.at[t], values_ref.at[t], value_sems.at[t])
        for t in range(values_ref.shape[0])
    ]
    for load in loads:
        load.wait()
    for fill in fills:
        fill.start()
    for h in range(2):
        rows = slice(h * half, (h + 1) * half)
        column = jnp.transpose(jnp.broadcast_to(inv_ref[h : h + 1, :], (half, half)))
        scaled = column * features_ref[rows, :].astype(jnp.float32)
        out_ref[me, rows, :] = scaled.astype(out_ref.dtype)
    met()
    sends = []
    neighbours = {"z": (zp, zm), "x": (xp, xm)}

    def rows_of(part):
        return pl.ds(PARTS[part][0], PARTS[part][1])

    def remote(slot, part, peer, n):
        return pltpu.make_async_remote_copy(
            src_ref=out_ref.at[slot, rows_of(part)],
            dst_ref=out_ref.at[slot, rows_of(part)],
            send_sem=send_sems.at[n],
            recv_sem=recv_sems.at[slot, part],
            device_id={"section": peer},
            device_id_type=MESH,
        )

    def send(slot, part, axis, way):
        sends.append(remote(slot, part, neighbours[axis][way], len(sends)))
        sends[-1].start()

    for turn in range(2):
        for part in range(4):
            axis = PARTS[part][2][turn]
            for way in ((0, 1), (1, 0))[PARTS[part][3]]:
                send(me, part, axis, way)

    def when(item):
        part, dx, dz = item
        x_hops, z_hops = min(dx, 4 - dx), min(dz, 4 - dz)
        if PARTS[part][2] == "zx":
            return 3.6 * z_hops + 2.4 * x_hops, part
        return 2.0 * x_hops + 3.4 * z_hops, part

    items = [
        (part, dx, dz) for part in range(4) for dx in range(4) for dz in range(4) if dx or dz
    ]
    for part, dx, dz in sorted(items, key=when):
        slot = sec(dx, dz)
        remote(slot, part, zp, 0).wait_recv()
        early, late = PARTS[part][2]
        way = PARTS[part][3]
        moved = {"x": dx, "z": dz}
        source = (3, 1)[way]
        if moved[late] == 0:
            if moved[early] == source:
                send(slot, part, early, way)
            send(slot, part, late, way)
            send(slot, part, late, 1 - way)
        elif moved[late] == source:
            send(slot, part, late, way)
    for fill in fills:
        fill.wait()
    for copy in sends:
        copy.wait_send()


def tiles_kernel(
    rows_hbm, cols_hbm, counts_hbm, pieces_ref, values_ref, out_ref,
    rows_ref, cols_ref, counts_ref, total, sems,
):
    loads = [
        pltpu.make_async_copy(source, target, sems.at[i])
        for i, (source, target) in enumerate(
            ((rows_hbm, rows_ref), (cols_hbm, cols_ref), (counts_hbm, counts_ref))
        )
    ]
    for load in loads:
        load.start()
    caps, sections = rows_ref.shape
    tile = total.shape[1]
    tile_rows = total.shape[0] - 1
    total[...] = jnp.zeros_like(total)
    for load in loads:
        load.wait()

    def body(t, carry):
        right = jnp.concatenate([pieces_ref[t, 0:tile, :], pieces_ref[t, tile : 2 * tile, :]], axis=1)
        left = values_ref[t].reshape(caps * tile, tile)
        both = jnp.dot(left, right, preferred_element_type=jnp.float32)
        for k in range(caps):
            row = jnp.where(k < counts_ref[0, t], rows_ref[k, t], tile_rows)
            part = both[k * tile : (k + 1) * tile, :]
            total[row] += jnp.where(cols_ref[k, t] == 0, part[:, :tile], part[:, tile:])
        return carry

    lax.fori_loop(0, sections, body, 0)
    for core in range(2):
        for y in range(8):
            for z in range(2):
                for h in range(2):
                    out_ref[core, y, z, h] = total[((z * 8 + y) * 2 + core) * 2 + h].astype(
                        out_ref.dtype
                    )


def scatter_kernel(
    part_ref, out_ref, mate, first0, runs0, first1, runs1, zout, zin,
    mate_send, mate_recv, send0, recv0, send1, recv1, z_send, z_recv,
):
    me = lax.axis_index("rep")
    core, y, z = me % 2, (me // 2) % 8, me // 16
    tile = out_ref.shape[0] // 2
    f32, bf16 = jnp.float32, jnp.bfloat16

    def rep(zz, yy, cc):
        return (zz * 8 + yy % 8) * 2 + cc

    other = rep(z, y, 1 - core)
    steps = (rep(z, y + 1, core), rep(z, y + 7, core))
    across = rep(1 - z, y, core)
    greet("rep", (other, steps[0], steps[1], across))()
    started = []

    def send(source, target, send_sem, recv_sem, peer):
        copy = pltpu.make_async_remote_copy(
            src_ref=source,
            dst_ref=target,
            send_sem=send_sem,
            recv_sem=recv_sem,
            device_id={"rep": peer},
            device_id_type=MESH,
        )
        copy.start()
        started.append(copy)
        return copy

    order = (4, 3, 5, 2, 6, 1, 7, 0)
    swaps, swapped = {}, set()
    for dy in order:
        at = (y + dy) % 8
        swaps[dy] = send(
            part_ref.at[1 - core, at], mate.at[at], mate_send.at[dy], mate_recv.at[dy], other
        )

    def term(dy, zi, h):
        dy = dy % 8
        if dy not in swapped:
            swapped.add(dy)
            swaps[dy].wait_recv()
        at = (y + dy) % 8
        zz = 1 - z if zi == 0 else z
        return part_ref[core, at, zz, h].astype(f32) + mate[at, zz, h].astype(f32)

    crosses = {}

    def cross(dy):
        zout[dy] = term(dy, 0, 1).astype(bf16)
        crosses[dy] = send(zout.at[dy], zin.at[dy], z_send.at[dy], z_recv.at[dy], across)

    def term1(dy):
        dy = dy % 8
        crosses[dy].wait_recv()
        return term(dy, 1, 1) + zin[dy].astype(f32)

    copies = {}

    def hop0(d, s):
        length = 3 + d
        for zi in range(2):
            value = term((length - s) * (1 - 2 * d), zi, 0)
            if s == 0:
                buf = first0.at[d, zi]
            else:
                copies[0, d, zi, s - 1].wait_recv()
                buf = runs0.at[d, zi, s - 1]
                value = value + buf[...].astype(f32)
            buf[...] = value.astype(bf16)
            copies[0, d, zi, s] = send(
                buf, runs0.at[d, zi, s], send0.at[d, zi, s], recv0.at[d, zi, s], steps[d]
            )

    def hop1(d, s):
        length = 4 - d
        value = term1((length - s) * (1 - 2 * d))
        if s == 0:
            buf = first1.at[d]
        else:
            copies[1, d, s - 1].wait_recv()
            buf = runs1.at[d, s - 1]
            value = value + buf[...].astype(f32)
        buf[...] = value.astype(bf16)
        copies[1, d, s] = send(buf, runs1.at[d, s], send1.at[d, s], recv1.at[d, s], steps[d])

    hop0(1, 0)
    cross(4)
    hop0(0, 0)
    for dy in order[1:]:
        cross(dy)
    hop0(1, 1)
    hop0(0, 1)
    hop1(0, 0)
    hop1(1, 0)
    hop0(1, 2)
    hop0(0, 2)
    hop1(0, 1)
    hop1(1, 1)
    hop0(1, 3)
    hop1(0, 2)
    hop1(1, 2)

    def gathered0(zi):
        value = term(0, zi, 0)
        for d in range(2):
            copies[0, d, zi, 2 + d].wait_recv()
            value = value + runs0[d, zi, 2 + d].astype(f32)
        return value

    zout[8] = gathered0(0).astype(bf16)
    last = send(zout.at[8], zin.at[8], z_send.at[8], z_recv.at[8], across)
    hop1(0, 3)
    mine = gathered0(1)
    value = term1(0)
    for d in range(2):
        copies[1, d, 3 - d].wait_recv()
        value = value + runs1[d, 3 - d].astype(f32)
    out_ref[tile:, :] = value
    last.wait_recv()
    out_ref[:tile, :] = mine + zin[8].astype(f32)
    for copy in started:
        copy.wait_send()


def shards(
    features, inv_degree, weight, bias_vector, tile_values, tile_rows, tile_cols, tile_counts
):
    rows_dev, width = features.shape
    sections, caps, tile = tile_values.shape[1:4]
    vmem = pl.BlockSpec(memory_space=pltpu.VMEM)
    hbm = pl.BlockSpec(memory_space=pltpu.HBM)
    bf16, f32 = jnp.bfloat16, jnp.float32
    dma = pltpu.SemaphoreType.DMA
    pieces, values = pl.pallas_call(
        gather_kernel,
        out_shape=(
            pltpu.VMEM((16, rows_dev, width), bf16),
            pltpu.VMEM(tile_values.shape[1:], bf16),
        ),
        in_specs=[hbm, hbm, hbm],
        out_specs=(vmem, vmem),
        scratch_shapes=[
            pltpu.VMEM((rows_dev, width), bf16),
            pltpu.VMEM((2, rows_dev // 2), f32),
            dma((60,)),
            dma((16, 4)),
            dma((2,)),
            dma((sections,)),
        ],
        compiler_params=pltpu.CompilerParams(
            collective_id=0, has_side_effects=True, vmem_limit_bytes=57 * MIB
        ),
        cost_estimate=pl.CostEstimate(flops=0, bytes_accessed=48 * MIB, transcendentals=0),
        name="gather_pieces",
    )(features, inv_degree.reshape(2, rows_dev // 2), tile_values[0])
    partial = pl.pallas_call(
        tiles_kernel,
        out_shape=jax.ShapeDtypeStruct((2, 8, 2, 2, tile, width), bf16),
        in_specs=[hbm, hbm, hbm, vmem, vmem],
        out_specs=vmem,
        scratch_shapes=[
            pltpu.SMEM((caps, sections), jnp.int32),
            pltpu.SMEM((caps, sections), jnp.int32),
            pltpu.SMEM((1, sections), jnp.int32),
            pltpu.VMEM((65, tile, width), f32),
            dma((3,)),
        ],
        compiler_params=pltpu.CompilerParams(vmem_limit_bytes=20 * MIB),
        name="tile_products",
    )(tile_rows[0].T, tile_cols[0].T, tile_counts, pieces, values)
    summed = pl.pallas_call(
        scatter_kernel,
        out_shape=jax.ShapeDtypeStruct((rows_dev, width), f32),
        in_specs=[vmem],
        out_specs=vmem,
        scratch_shapes=[
            pltpu.VMEM((8, 2, 2, tile, width), bf16),
            pltpu.VMEM((2, 2, tile, width), bf16),
            pltpu.VMEM((2, 2, 4, tile, width), bf16),
            pltpu.VMEM((2, tile, width), bf16),
            pltpu.VMEM((2, 4, tile, width), bf16),
            pltpu.VMEM((9, tile, width), bf16),
            pltpu.VMEM((9, tile, width), bf16),
            dma((8,)),
            dma((8,)),
            dma((2, 2, 4)),
            dma((2, 2, 4)),
            dma((2, 4)),
            dma((2, 4)),
            dma((9,)),
            dma((9,)),
        ],
        compiler_params=pltpu.CompilerParams(
            collective_id=1, has_side_effects=True, vmem_limit_bytes=16 * MIB
        ),
        cost_estimate=pl.CostEstimate(flops=0, bytes_accessed=48 * MIB, transcendentals=0),
        name="scatter_sums",
    )(partial)
    normed = (inv_degree[:, None] * summed).astype(bf16)
    hidden = jnp.dot(normed, weight, preferred_element_type=f32) + bias_vector
    return jnp.maximum(hidden, 0.0).astype(bf16)


def solution(mesh):
    return jax.shard_map(
        shards,
        mesh=mesh,
        in_specs=(
            P(("section", "rep"), None),
            P(("section", "rep")),
            P(),
            P(),
            P(("section", "rep"), None, None, None, None),
            P(("section", "rep"), None, None),
            P(("section", "rep"), None, None),
            P(("section", "rep"), None),
        ),
        out_specs=P(("section", "rep"), None),
        check_vma=False,
    )
```

```python
import jax
import jax.numpy as jnp
from jax import lax
from jax.experimental import pallas as pl
from jax.experimental.pallas import tpu as pltpu
from jax.sharding import PartitionSpec as P

MESH = pl.DeviceIdType.MESH
MIB = 1024 * 1024


def greet(axis, peers):
    barrier = pltpu.get_barrier_semaphore()
    for peer in peers:
        pl.semaphore_signal(barrier, inc=1, device_id={axis: peer}, device_id_type=MESH)
    return lambda: pl.semaphore_wait(barrier, len(peers))


def gather_kernel(
    features_hbm, inv_hbm, values_hbm, products_ref,
    out_ref, values_ref, features_ref, inv_ref, send_sems, recv_sems, load_sems, value_sems,
):
    me = lax.axis_index("section")
    x, z = me // 4, me % 4
    half = features_ref.shape[0] // 2

    def sec(dx, dz):
        return ((x + dx) % 4) * 4 + (z + dz) % 4

    zp, zm, xp, xm = sec(0, 1), sec(0, 3), sec(1, 0), sec(3, 0)
    met = greet("section", (zp, zm, xp, xm))
    loads = [
        pltpu.make_async_copy(features_hbm, features_ref, load_sems.at[0]),
        pltpu.make_async_copy(inv_hbm, inv_ref, load_sems.at[1]),
    ]
    for load in loads:
        load.start()
    fills = [
        pltpu.make_async_copy(values_hbm.at[t], values_ref.at[t], value_sems.at[t])
        for t in range(values_ref.shape[0])
    ]
    for load in loads:
        load.wait()
    for fill in fills:
        fill.start()
    for h in range(2):
        rows = slice(h * half, (h + 1) * half)
        column = jnp.transpose(jnp.broadcast_to(inv_ref[h : h + 1, :], (half, half)))
        scaled = column * features_ref[rows, :].astype(jnp.float32)
        out_ref[me, rows, :] = scaled.astype(out_ref.dtype)
    met()
    sends = []

    def send(slot, h, peer):
        rows = pl.ds(h * half, half)
        copy = pltpu.make_async_remote_copy(
            src_ref=out_ref.at[slot, rows],
            dst_ref=out_ref.at[slot, rows],
            send_sem=send_sems.at[len(sends)],
            recv_sem=recv_sems.at[slot, h],
            device_id={"section": peer},
            device_id_type=MESH,
        )
        copy.start()
        sends.append(copy)

    waited = set()

    def need(dx, dz, h):
        if (dx, dz, h) in waited:
            return
        waited.add((dx, dz, h))
        slot, rows = sec(dx, dz), pl.ds(h * half, half)
        pltpu.make_async_remote_copy(
            src_ref=out_ref.at[slot, rows],
            dst_ref=out_ref.at[slot, rows],
            send_sem=send_sems.at[0],
            recv_sem=recv_sems.at[slot, h],
            device_id={"section": zp},
            device_id_type=MESH,
        ).wait_recv()

    def product(dx, dz):
        if (dx, dz) != (0, 0):
            need(dx, dz, 0)
            need(dx, dz, 1)
        slot = sec(dx, dz)
        caps, tile = values_ref.shape[1:3]
        right = jnp.concatenate([out_ref[slot, 0:tile, :], out_ref[slot, tile:, :]], axis=1)
        left = values_ref[slot].reshape(caps * tile, tile)
        both = jnp.dot(left, right, preferred_element_type=jnp.float32)
        for c in range(2):
            products_ref[slot, c] = both[:, c * tile : (c + 1) * tile].reshape(caps, tile, tile)

    for h, peer in ((0, zp), (1, zm), (1, zp), (0, zm), (0, xp), (1, xm), (1, xp), (0, xm)):
        send(me, h, peer)
    for fill in fills:
        fill.wait()
    product(0, 0)
    need(0, 3, 0)
    send(sec(0, 3), 0, zp)
    need(0, 1, 1)
    send(sec(0, 1), 1, zm)
    send(sec(0, 3), 0, xp)
    send(sec(0, 1), 1, xm)
    need(3, 0, 0)
    send(sec(3, 0), 0, xp)
    need(1, 0, 1)
    send(sec(1, 0), 1, xm)
    send(sec(0, 1), 1, xp)
    send(sec(0, 3), 0, xm)
    need(0, 3, 1)
    send(sec(0, 3), 1, xp)
    send(sec(0, 3), 1, xm)
    need(0, 1, 0)
    send(sec(0, 1), 0, xp)
    send(sec(0, 1), 0, xm)
    product(3, 0)
    product(1, 0)
    product(0, 3)
    product(0, 1)
    need(3, 3, 0)
    send(sec(3, 3), 0, xp)
    need(1, 1, 1)
    send(sec(1, 1), 1, xm)
    need(0, 2, 0)
    send(sec(0, 2), 0, xp)
    send(sec(0, 2), 0, xm)
    need(0, 2, 1)
    send(sec(0, 2), 1, xm)
    send(sec(0, 2), 1, xp)
    product(0, 2)
    need(1, 3, 1)
    send(sec(1, 3), 1, xm)
    need(3, 1, 0)
    send(sec(3, 1), 0, xp)
    product(2, 0)
    product(3, 3)
    product(1, 1)
    need(3, 2, 0)
    send(sec(3, 2), 0, xp)
    need(1, 2, 1)
    send(sec(1, 2), 1, xm)
    for dx, dz in ((1, 3), (3, 1), (2, 3), (2, 1), (3, 2), (1, 2), (2, 2)):
        product(dx, dz)
    for copy in sends:
        copy.wait_send()


def tiles_kernel(
    rows_hbm, cols_hbm, counts_hbm, products_ref, out_ref,
    rows_ref, cols_ref, counts_ref, total, sems,
):
    loads = [
        pltpu.make_async_copy(source, target, sems.at[i])
        for i, (source, target) in enumerate(
            ((rows_hbm, rows_ref), (cols_hbm, cols_ref), (counts_hbm, counts_ref))
        )
    ]
    for load in loads:
        load.start()
    caps, sections = rows_ref.shape
    tile_rows = total.shape[0] - 1
    total[...] = jnp.zeros_like(total)
    for load in loads:
        load.wait()

    def body(t, carry):
        for k in range(caps):
            live = k < counts_ref[0, t]
            row = jnp.where(live, rows_ref[k, t], tile_rows)
            col = jnp.where(live, cols_ref[k, t], 0)
            total[row] += products_ref[t, col, k]
        return carry

    lax.fori_loop(0, sections, body, 0)
    for core in range(2):
        for y in range(8):
            for z in range(2):
                for h in range(2):
                    out_ref[core, y, z, h] = total[((z * 8 + y) * 2 + core) * 2 + h].astype(
                        out_ref.dtype
                    )


def scatter_kernel(
    part_ref, out_ref, mate, first, runs, zout, zin,
    mate_send, mate_recv, run_send, run_recv, z_send, z_recv,
):
    me = lax.axis_index("rep")
    core, y, z = me % 2, (me // 2) % 8, me // 16
    tile = out_ref.shape[0] // 2

    def rep(zz, yy, cc):
        return (zz * 8 + yy % 8) * 2 + cc

    other = rep(z, y, 1 - core)
    steps = (rep(z, y + 1, core), rep(z, y + 7, core))
    across = rep(1 - z, y, core)
    greet("rep", (other, steps[0], steps[1], across))()

    swaps = {}
    for dy in (4, 3, 5, 2, 6, 1, 7, 0):
        at = (y + dy) % 8
        swaps[dy] = pltpu.make_async_remote_copy(
            src_ref=part_ref.at[1 - core, at],
            dst_ref=mate.at[at],
            send_sem=mate_send.at[dy],
            recv_sem=mate_recv.at[dy],
            device_id={"rep": other},
            device_id_type=MESH,
        )
        swaps[dy].start()
    swapped = set()

    def term(dy, zi, h):
        dy = dy % 8
        if dy not in swapped:
            swapped.add(dy)
            swaps[dy].wait_recv()
        at = (y + dy) % 8
        zz = 1 - z if zi == 0 else z
        return part_ref[core, at, zz, h].astype(jnp.float32) + mate[at, zz, h].astype(jnp.float32)

    def hops(d, h):
        return 4 if d != h else 3

    copies = {}
    for s in range(4):
        for zi in range(2):
            for d, h in ((0, 1), (1, 0), (0, 0), (1, 1)):
                length = hops(d, h)
                if s >= length:
                    continue
                dy = (length - s) * (1 - 2 * d)
                value = term(dy, zi, h)
                if s == 0:
                    buf = first.at[d, h, zi]
                else:
                    copies[d, h, zi, s - 1].wait_recv()
                    buf = runs.at[d, h, zi, s - 1]
                    value = value + buf[...].astype(jnp.float32)
                buf[...] = value.astype(jnp.bfloat16)
                copies[d, h, zi, s] = pltpu.make_async_remote_copy(
                    src_ref=buf,
                    dst_ref=runs.at[d, h, zi, s],
                    send_sem=run_send.at[d, h, zi, s],
                    recv_sem=run_recv.at[d, h, zi, s],
                    device_id={"rep": steps[d]},
                    device_id_type=MESH,
                )
                copies[d, h, zi, s].start()

    def gathered(zi, h):
        value = term(0, zi, h)
        for d in range(2):
            last = hops(d, h) - 1
            copies[d, h, zi, last].wait_recv()
            value = value + runs[d, h, zi, last].astype(jnp.float32)
        return value

    crosses = []
    for h in range(2):
        zout[h] = gathered(0, h).astype(jnp.bfloat16)
        crosses.append(
            pltpu.make_async_remote_copy(
                src_ref=zout.at[h],
                dst_ref=zin.at[h],
                send_sem=z_send.at[h],
                recv_sem=z_recv.at[h],
                device_id={"rep": across},
                device_id_type=MESH,
            )
        )
        crosses[h].start()
    mine = [gathered(1, h) for h in range(2)]
    for h in range(2):
        crosses[h].wait_recv()
        out_ref[h * tile : (h + 1) * tile, :] = mine[h] + zin[h].astype(jnp.float32)
    for copy in list(swaps.values()) + list(copies.values()) + crosses:
        copy.wait_send()


def shards(
    features, inv_degree, weight, bias_vector, tile_values, tile_rows, tile_cols, tile_counts
):
    rows_dev, width = features.shape
    sections, caps, tile = tile_values.shape[1:4]
    vmem = pl.BlockSpec(memory_space=pltpu.VMEM)
    hbm = pl.BlockSpec(memory_space=pltpu.HBM)
    bf16, f32 = jnp.bfloat16, jnp.float32
    dma = pltpu.SemaphoreType.DMA
    products = pl.pallas_call(
        gather_kernel,
        out_shape=pltpu.VMEM((sections, 2, caps, tile, width), f32),
        in_specs=[hbm, hbm, hbm],
        out_specs=vmem,
        scratch_shapes=[
            pltpu.VMEM((sections, rows_dev, width), bf16),
            pltpu.VMEM(tile_values.shape[1:], bf16),
            pltpu.VMEM((rows_dev, width), bf16),
            pltpu.VMEM((2, rows_dev // 2), f32),
            dma((30,)),
            dma((16, 2)),
            dma((2,)),
            dma((sections,)),
        ],
        compiler_params=pltpu.CompilerParams(
            collective_id=0, has_side_effects=True, vmem_limit_bytes=46 * MIB
        ),
        cost_estimate=pl.CostEstimate(flops=0, bytes_accessed=48 * MIB, transcendentals=0),
        name="gather_pieces",
    )(features, inv_degree.reshape(2, rows_dev // 2), tile_values[0])
    partial = pl.pallas_call(
        tiles_kernel,
        out_shape=jax.ShapeDtypeStruct((2, 8, 2, 2, tile, width), bf16),
        in_specs=[hbm, hbm, hbm, vmem],
        out_specs=vmem,
        scratch_shapes=[
            pltpu.SMEM((caps, sections), jnp.int32),
            pltpu.SMEM((caps, sections), jnp.int32),
            pltpu.SMEM((1, sections), jnp.int32),
            pltpu.VMEM((65, tile, width), f32),
            dma((3,)),
        ],
        compiler_params=pltpu.CompilerParams(vmem_limit_bytes=20 * MIB),
        name="tile_products",
    )(tile_rows[0].T, tile_cols[0].T, tile_counts, products)
    summed = pl.pallas_call(
        scatter_kernel,
        out_shape=jax.ShapeDtypeStruct((rows_dev, width), f32),
        in_specs=[vmem],
        out_specs=vmem,
        scratch_shapes=[
            pltpu.VMEM((8, 2, 2, tile, width), bf16),
            pltpu.VMEM((2, 2, 2, tile, width), bf16),
            pltpu.VMEM((2, 2, 2, 4, tile, width), bf16),
            pltpu.VMEM((2, tile, width), bf16),
            pltpu.VMEM((2, tile, width), bf16),
            dma((8,)),
            dma((8,)),
            dma((2, 2, 2, 4)),
            dma((2, 2, 2, 4)),
            dma((2,)),
            dma((2,)),
        ],
        compiler_params=pltpu.CompilerParams(
            collective_id=1, has_side_effects=True, vmem_limit_bytes=16 * MIB
        ),
        cost_estimate=pl.CostEstimate(flops=0, bytes_accessed=48 * MIB, transcendentals=0),
        name="scatter_sums",
    )(partial)
    normed = (inv_degree[:, None] * summed).astype(bf16)
    hidden = jnp.dot(normed, weight, preferred_element_type=f32) + bias_vector
    return jnp.maximum(hidden, 0.0).astype(bf16)


def solution(mesh):
    return jax.shard_map(
        shards,
        mesh=mesh,
        in_specs=(
            P(("section", "rep"), None),
            P(("section", "rep")),
            P(),
            P(),
            P(("section", "rep"), None, None, None, None),
            P(("section", "rep"), None, None),
            P(("section", "rep"), None, None),
            P(("section", "rep"), None),
        ),
        out_specs=P(("section", "rep"), None),
        check_vma=False,
    )
```

```python
import jax
import jax.numpy as jnp
from jax import lax
from jax.experimental import pallas as pl
from jax.experimental.pallas import tpu as pltpu
from jax.sharding import PartitionSpec as P

MESH = pl.DeviceIdType.MESH
MIB = 1024 * 1024


def greet(axis, peers):
    barrier = pltpu.get_barrier_semaphore()
    for peer in peers:
        pl.semaphore_signal(barrier, inc=1, device_id={axis: peer}, device_id_type=MESH)
    return lambda: pl.semaphore_wait(barrier, len(peers))


def gather_kernel(
    features_hbm, inv_hbm, values_hbm, products_ref,
    out_ref, values_ref, features_ref, inv_ref, send_sems, recv_sems, load_sems, value_sems,
):
    me = lax.axis_index("section")
    x, z = me // 4, me % 4
    half = features_ref.shape[0] // 2

    def sec(dx, dz):
        return ((x + dx) % 4) * 4 + (z + dz) % 4

    zp, zm, xp, xm = sec(0, 1), sec(0, 3), sec(1, 0), sec(3, 0)
    met = greet("section", (zp, zm, xp, xm))
    loads = [
        pltpu.make_async_copy(features_hbm, features_ref, load_sems.at[0]),
        pltpu.make_async_copy(inv_hbm, inv_ref, load_sems.at[1]),
    ]
    for load in loads:
        load.start()
    fills = [
        pltpu.make_async_copy(values_hbm.at[t], values_ref.at[t], value_sems.at[t])
        for t in range(values_ref.shape[0])
    ]
    for load in loads:
        load.wait()
    for fill in fills:
        fill.start()
    for h in range(2):
        rows = slice(h * half, (h + 1) * half)
        column = jnp.transpose(jnp.broadcast_to(inv_ref[h : h + 1, :], (half, half)))
        scaled = column * features_ref[rows, :].astype(jnp.float32)
        out_ref[me, rows, :] = scaled.astype(out_ref.dtype)
    met()
    sends = []

    def send(slot, h, peer):
        rows = pl.ds(h * (half // 2), half // 2)
        copy = pltpu.make_async_remote_copy(
            src_ref=out_ref.at[slot, rows],
            dst_ref=out_ref.at[slot, rows],
            send_sem=send_sems.at[len(sends)],
            recv_sem=recv_sems.at[slot, h],
            device_id={"section": peer},
            device_id_type=MESH,
        )
        copy.start()
        sends.append(copy)

    waited = set()

    def need(dx, dz, h):
        if (dx, dz, h) in waited:
            return
        waited.add((dx, dz, h))
        slot, rows = sec(dx, dz), pl.ds(h * (half // 2), half // 2)
        pltpu.make_async_remote_copy(
            src_ref=out_ref.at[slot, rows],
            dst_ref=out_ref.at[slot, rows],
            send_sem=send_sems.at[0],
            recv_sem=recv_sems.at[slot, h],
            device_id={"section": zp},
            device_id_type=MESH,
        ).wait_recv()

    def product(dx, dz):
        if (dx, dz) != (0, 0):
            for q in range(4):
                need(dx, dz, q)
        slot = sec(dx, dz)
        caps, tile = values_ref.shape[1:3]
        right = jnp.concatenate([out_ref[slot, 0:tile, :], out_ref[slot, tile:, :]], axis=1)
        left = values_ref[slot].reshape(caps * tile, tile)
        both = jnp.dot(left, right, preferred_element_type=jnp.float32)
        for c in range(2):
            products_ref[slot, c] = both[:, c * tile : (c + 1) * tile].reshape(caps, tile, tile)

    def relay(*items):
        for g in range(2):
            for dx, dz, h, peers in items:
                if (dx, dz) != (0, 0):
                    need(dx, dz, 2 * h + g)
                for peer in peers:
                    send(sec(dx, dz), 2 * h + g, peer)

    relay((0, 0, 0, (zp,)), (0, 0, 1, (zm,)))
    relay((0, 0, 1, (zp,)), (0, 0, 0, (zm,)))
    relay((0, 0, 0, (xp,)), (0, 0, 1, (xm,)))
    relay((0, 0, 1, (xp,)), (0, 0, 0, (xm,)))
    for fill in fills:
        fill.wait()
    product(0, 0)
    relay((0, 3, 0, (zp, xp)), (0, 1, 1, (zm, xm)))
    relay((3, 0, 0, (xp,)), (1, 0, 1, (xm,)))
    relay((0, 1, 1, (xp,)), (0, 3, 0, (xm,)))
    relay((0, 3, 1, (xp, xm)), (0, 1, 0, (xp, xm)))
    product(3, 0)
    product(1, 0)
    product(0, 3)
    product(0, 1)
    relay((3, 3, 0, (xp,)), (1, 1, 1, (xm,)))
    relay((0, 2, 0, (xp, xm)), (0, 2, 1, (xm, xp)))
    product(0, 2)
    relay((1, 3, 1, (xm,)), (3, 1, 0, (xp,)))
    product(2, 0)
    product(3, 3)
    product(1, 1)
    relay((3, 2, 0, (xp,)), (1, 2, 1, (xm,)))
    for dx, dz in ((1, 3), (3, 1), (2, 3), (2, 1), (3, 2), (1, 2), (2, 2)):
        product(dx, dz)
    for copy in sends:
        copy.wait_send()


def tiles_kernel(
    rows_hbm, cols_hbm, counts_hbm, products_ref, out_ref,
    rows_ref, cols_ref, counts_ref, total, sems,
):
    loads = [
        pltpu.make_async_copy(source, target, sems.at[i])
        for i, (source, target) in enumerate(
            ((rows_hbm, rows_ref), (cols_hbm, cols_ref), (counts_hbm, counts_ref))
        )
    ]
    for load in loads:
        load.start()
    caps, sections = rows_ref.shape
    tile_rows = total.shape[0] - 1
    total[...] = jnp.zeros_like(total)
    for load in loads:
        load.wait()

    def body(t, carry):
        for k in range(caps):
            live = k < counts_ref[0, t]
            row = jnp.where(live, rows_ref[k, t], tile_rows)
            col = jnp.where(live, cols_ref[k, t], 0)
            total[row] += products_ref[t, col, k]
        return carry

    lax.fori_loop(0, sections, body, 0)
    for core in range(2):
        for y in range(8):
            for z in range(2):
                for h in range(4):
                    rows = slice(h % 2 * 64, h % 2 * 64 + 64)
                    out_ref[core, y, z, h] = total[
                        ((z * 8 + y) * 2 + core) * 2 + h // 2, rows, :
                    ].astype(out_ref.dtype)


def scatter_kernel(
    part_ref, out_ref, mate, first, runs, zout, zin,
    mate_send, mate_recv, run_send, run_recv, z_send, z_recv,
):
    me = lax.axis_index("rep")
    core, y, z = me % 2, (me // 2) % 8, me // 16
    part = out_ref.shape[0] // 4

    def rep(zz, yy, cc):
        return (zz * 8 + yy % 8) * 2 + cc

    other = rep(z, y, 1 - core)
    steps = (rep(z, y + 1, core), rep(z, y + 7, core))
    across = rep(1 - z, y, core)
    greet("rep", (other, steps[0], steps[1], across))()

    swaps = {}
    for dy in (4, 3, 5, 2, 6, 1, 7, 0):
        at = (y + dy) % 8
        swaps[dy] = pltpu.make_async_remote_copy(
            src_ref=part_ref.at[1 - core, at],
            dst_ref=mate.at[at],
            send_sem=mate_send.at[dy],
            recv_sem=mate_recv.at[dy],
            device_id={"rep": other},
            device_id_type=MESH,
        )
        swaps[dy].start()
    swapped = set()

    def term(dy, zi, h):
        dy = dy % 8
        if dy not in swapped:
            swapped.add(dy)
            swaps[dy].wait_recv()
        at = (y + dy) % 8
        zz = 1 - z if zi == 0 else z
        return part_ref[core, at, zz, h].astype(jnp.float32) + mate[at, zz, h].astype(jnp.float32)

    def hops(d, h):
        return 4 if d != h // 2 else 3

    copies = {}
    for s in range(4):
        for zi in range(2):
            for d, h in ((0, 2), (1, 0), (0, 3), (1, 1), (0, 0), (1, 2), (0, 1), (1, 3)):
                length = hops(d, h)
                if s >= length:
                    continue
                dy = (length - s) * (1 - 2 * d)
                value = term(dy, zi, h)
                if s == 0:
                    buf = first.at[d, h, zi]
                else:
                    copies[d, h, zi, s - 1].wait_recv()
                    buf = runs.at[d, h, zi, s - 1]
                    value = value + buf[...].astype(jnp.float32)
                buf[...] = value.astype(jnp.bfloat16)
                copies[d, h, zi, s] = pltpu.make_async_remote_copy(
                    src_ref=buf,
                    dst_ref=runs.at[d, h, zi, s],
                    send_sem=run_send.at[d, h, zi, s],
                    recv_sem=run_recv.at[d, h, zi, s],
                    device_id={"rep": steps[d]},
                    device_id_type=MESH,
                )
                copies[d, h, zi, s].start()

    def gathered(zi, h):
        value = term(0, zi, h)
        for d in range(2):
            last = hops(d, h) - 1
            copies[d, h, zi, last].wait_recv()
            value = value + runs[d, h, zi, last].astype(jnp.float32)
        return value

    crosses = []
    for h in range(4):
        zout[h] = gathered(0, h).astype(jnp.bfloat16)
        crosses.append(
            pltpu.make_async_remote_copy(
                src_ref=zout.at[h],
                dst_ref=zin.at[h],
                send_sem=z_send.at[h],
                recv_sem=z_recv.at[h],
                device_id={"rep": across},
                device_id_type=MESH,
            )
        )
        crosses[h].start()
    mine = [gathered(1, h) for h in range(4)]
    for h in range(4):
        crosses[h].wait_recv()
        out_ref[h * part : (h + 1) * part, :] = mine[h] + zin[h].astype(jnp.float32)
    for copy in list(swaps.values()) + list(copies.values()) + crosses:
        copy.wait_send()


def shards(
    features, inv_degree, weight, bias_vector, tile_values, tile_rows, tile_cols, tile_counts
):
    rows_dev, width = features.shape
    sections, caps, tile = tile_values.shape[1:4]
    vmem = pl.BlockSpec(memory_space=pltpu.VMEM)
    hbm = pl.BlockSpec(memory_space=pltpu.HBM)
    bf16, f32 = jnp.bfloat16, jnp.float32
    dma = pltpu.SemaphoreType.DMA
    products = pl.pallas_call(
        gather_kernel,
        out_shape=pltpu.VMEM((sections, 2, caps, tile, width), f32),
        in_specs=[hbm, hbm, hbm],
        out_specs=vmem,
        scratch_shapes=[
            pltpu.VMEM((sections, rows_dev, width), bf16),
            pltpu.VMEM(tile_values.shape[1:], bf16),
            pltpu.VMEM((rows_dev, width), bf16),
            pltpu.VMEM((2, rows_dev // 2), f32),
            dma((60,)),
            dma((16, 4)),
            dma((2,)),
            dma((sections,)),
        ],
        compiler_params=pltpu.CompilerParams(
            collective_id=0, has_side_effects=True, vmem_limit_bytes=46 * MIB
        ),
        cost_estimate=pl.CostEstimate(flops=0, bytes_accessed=48 * MIB, transcendentals=0),
        name="gather_pieces",
    )(features, inv_degree.reshape(2, rows_dev // 2), tile_values[0])
    partial = pl.pallas_call(
        tiles_kernel,
        out_shape=jax.ShapeDtypeStruct((2, 8, 2, 4, tile // 2, width), bf16),
        in_specs=[hbm, hbm, hbm, vmem],
        out_specs=vmem,
        scratch_shapes=[
            pltpu.SMEM((caps, sections), jnp.int32),
            pltpu.SMEM((caps, sections), jnp.int32),
            pltpu.SMEM((1, sections), jnp.int32),
            pltpu.VMEM((65, tile, width), f32),
            dma((3,)),
        ],
        compiler_params=pltpu.CompilerParams(vmem_limit_bytes=20 * MIB),
        name="tile_products",
    )(tile_rows[0].T, tile_cols[0].T, tile_counts, products)
    summed = pl.pallas_call(
        scatter_kernel,
        out_shape=jax.ShapeDtypeStruct((rows_dev, width), f32),
        in_specs=[vmem],
        out_specs=vmem,
        scratch_shapes=[
            pltpu.VMEM((8, 2, 4, tile // 2, width), bf16),
            pltpu.VMEM((2, 4, 2, tile // 2, width), bf16),
            pltpu.VMEM((2, 4, 2, 4, tile // 2, width), bf16),
            pltpu.VMEM((4, tile // 2, width), bf16),
            pltpu.VMEM((4, tile // 2, width), bf16),
            dma((8,)),
            dma((8,)),
            dma((2, 4, 2, 4)),
            dma((2, 4, 2, 4)),
            dma((4,)),
            dma((4,)),
        ],
        compiler_params=pltpu.CompilerParams(
            collective_id=1, has_side_effects=True, vmem_limit_bytes=16 * MIB
        ),
        cost_estimate=pl.CostEstimate(flops=0, bytes_accessed=48 * MIB, transcendentals=0),
        name="scatter_sums",
    )(partial)
    normed = (inv_degree[:, None] * summed).astype(bf16)
    hidden = jnp.dot(normed, weight, preferred_element_type=f32) + bias_vector
    return jnp.maximum(hidden, 0.0).astype(bf16)


def solution(mesh):
    return jax.shard_map(
        shards,
        mesh=mesh,
        in_specs=(
            P(("section", "rep"), None),
            P(("section", "rep")),
            P(),
            P(),
            P(("section", "rep"), None, None, None, None),
            P(("section", "rep"), None, None),
            P(("section", "rep"), None, None),
            P(("section", "rep"), None),
        ),
        out_specs=P(("section", "rep"), None),
        check_vma=False,
    )
```

```python
import jax
import jax.numpy as jnp
from jax import lax
from jax.experimental import pallas as pl
from jax.experimental.pallas import tpu as pltpu
from jax.sharding import PartitionSpec as P

MESH = pl.DeviceIdType.MESH
MIB = 1024 * 1024


def greet(axis, peers):
    barrier = pltpu.get_barrier_semaphore()
    for peer in peers:
        pl.semaphore_signal(barrier, inc=1, device_id={axis: peer}, device_id_type=MESH)
    return lambda: pl.semaphore_wait(barrier, len(peers))


def gather_kernel(
    features_hbm, inv_hbm, values_hbm, products_ref,
    out_ref, values_ref, features_ref, inv_ref, send_sems, recv_sems, load_sems, value_sems,
):
    me = lax.axis_index("section")
    x, z = me // 4, me % 4
    half = features_ref.shape[0] // 2

    def sec(dx, dz):
        return ((x + dx) % 4) * 4 + (z + dz) % 4

    zp, zm, xp, xm = sec(0, 1), sec(0, 3), sec(1, 0), sec(3, 0)
    met = greet("section", (zp, zm, xp, xm))
    loads = [
        pltpu.make_async_copy(features_hbm, features_ref, load_sems.at[0]),
        pltpu.make_async_copy(inv_hbm, inv_ref, load_sems.at[1]),
    ]
    for load in loads:
        load.start()
    fills = [
        pltpu.make_async_copy(values_hbm.at[t], values_ref.at[t], value_sems.at[t])
        for t in range(values_ref.shape[0])
    ]
    for load in loads:
        load.wait()
    for fill in fills:
        fill.start()
    for h in range(2):
        rows = slice(h * half, (h + 1) * half)
        column = jnp.transpose(jnp.broadcast_to(inv_ref[h : h + 1, :], (half, half)))
        scaled = column * features_ref[rows, :].astype(jnp.float32)
        out_ref[me, rows, :] = scaled.astype(out_ref.dtype)
    met()
    sends = []

    def send(slot, h, peer):
        rows = pl.ds(h * (half // 2), half // 2)
        copy = pltpu.make_async_remote_copy(
            src_ref=out_ref.at[slot, rows],
            dst_ref=out_ref.at[slot, rows],
            send_sem=send_sems.at[len(sends)],
            recv_sem=recv_sems.at[slot, h],
            device_id={"section": peer},
            device_id_type=MESH,
        )
        copy.start()
        sends.append(copy)

    waited = set()

    def need(dx, dz, h):
        if (dx, dz, h) in waited:
            return
        waited.add((dx, dz, h))
        slot, rows = sec(dx, dz), pl.ds(h * (half // 2), half // 2)
        pltpu.make_async_remote_copy(
            src_ref=out_ref.at[slot, rows],
            dst_ref=out_ref.at[slot, rows],
            send_sem=send_sems.at[0],
            recv_sem=recv_sems.at[slot, h],
            device_id={"section": zp},
            device_id_type=MESH,
        ).wait_recv()

    def product(dx, dz):
        if (dx, dz) != (0, 0):
            for q in range(4):
                need(dx, dz, q)
        slot = sec(dx, dz)
        caps, tile = values_ref.shape[1:3]
        right = jnp.concatenate([out_ref[slot, 0:tile, :], out_ref[slot, tile:, :]], axis=1)
        left = values_ref[slot].reshape(caps * tile, tile)
        both = jnp.dot(left, right, preferred_element_type=jnp.float32)
        for c in range(2):
            products_ref[slot, c] = both[:, c * tile : (c + 1) * tile].reshape(caps, tile, tile)

    def relay(*items):
        for g in range(2):
            for dx, dz, h, peers in items:
                if (dx, dz) != (0, 0):
                    need(dx, dz, 2 * h + g)
                for peer in peers:
                    send(sec(dx, dz), 2 * h + g, peer)

    relay((0, 0, 0, (zp,)), (0, 0, 1, (zm,)))
    relay((0, 0, 1, (zp,)), (0, 0, 0, (zm,)))
    relay((0, 0, 0, (xp,)), (0, 0, 1, (xm,)))
    relay((0, 0, 1, (xp,)), (0, 0, 0, (xm,)))
    for fill in fills:
        fill.wait()
    product(0, 0)
    relay((0, 3, 0, (zp, xp)), (0, 1, 1, (zm, xm)))
    relay((3, 0, 0, (xp,)), (1, 0, 1, (xm,)))
    relay((0, 1, 1, (xp,)), (0, 3, 0, (xm,)))
    relay((0, 3, 1, (xp, xm)), (0, 1, 0, (xp, xm)))
    product(3, 0)
    product(1, 0)
    product(0, 3)
    product(0, 1)
    relay((3, 3, 0, (xp,)), (1, 1, 1, (xm,)))
    relay((0, 2, 0, (xp, xm)), (0, 2, 1, (xm, xp)))
    product(0, 2)
    relay((1, 3, 1, (xm,)), (3, 1, 0, (xp,)))
    product(2, 0)
    product(3, 3)
    product(1, 1)
    relay((3, 2, 0, (xp,)), (1, 2, 1, (xm,)))
    for dx, dz in ((1, 3), (3, 1), (2, 3), (2, 1), (3, 2), (1, 2), (2, 2)):
        product(dx, dz)
    for copy in sends:
        copy.wait_send()


def tiles_kernel(
    rows_hbm, cols_hbm, counts_hbm, products_ref, out_ref,
    rows_ref, cols_ref, counts_ref, total, sems,
):
    loads = [
        pltpu.make_async_copy(source, target, sems.at[i])
        for i, (source, target) in enumerate(
            ((rows_hbm, rows_ref), (cols_hbm, cols_ref), (counts_hbm, counts_ref))
        )
    ]
    for load in loads:
        load.start()
    caps, sections = rows_ref.shape
    tile_rows = total.shape[0] - 1
    total[...] = jnp.zeros_like(total)
    for load in loads:
        load.wait()

    def body(t, carry):
        for k in range(caps):
            live = k < counts_ref[0, t]
            row = jnp.where(live, rows_ref[k, t], tile_rows)
            col = jnp.where(live, cols_ref[k, t], 0)
            total[row] += products_ref[t, col, k]
        return carry

    lax.fori_loop(0, sections, body, 0)
    for core in range(2):
        for y in range(8):
            for z in range(2):
                for h in range(4):
                    rows = slice(h % 2 * 64, h % 2 * 64 + 64)
                    out_ref[core, y, z, h] = total[
                        ((z * 8 + y) * 2 + core) * 2 + h // 2, rows, :
                    ].astype(out_ref.dtype)


def scatter_kernel(
    part_ref, out_ref, mate, first, runs, zout, zin,
    mate_send, mate_recv, run_send, run_recv, z_send, z_recv,
):
    me = lax.axis_index("rep")
    core, y, z = me % 2, (me // 2) % 8, me // 16
    part = out_ref.shape[0] // 4

    def rep(zz, yy, cc):
        return (zz * 8 + yy % 8) * 2 + cc

    other = rep(z, y, 1 - core)
    steps = (rep(z, y + 1, core), rep(z, y + 7, core))
    across = rep(1 - z, y, core)
    greet("rep", (other, steps[0], steps[1], across))()

    swaps = {}
    for dy in (4, 3, 5, 2, 6, 1, 7, 0):
        at = (y + dy) % 8
        swaps[dy] = pltpu.make_async_remote_copy(
            src_ref=part_ref.at[1 - core, at],
            dst_ref=mate.at[at],
            send_sem=mate_send.at[dy],
            recv_sem=mate_recv.at[dy],
            device_id={"rep": other},
            device_id_type=MESH,
        )
        swaps[dy].start()
    swapped = set()

    def term(dy, zi, h):
        dy = dy % 8
        if dy not in swapped:
            swapped.add(dy)
            swaps[dy].wait_recv()
        at = (y + dy) % 8
        zz = 1 - z if zi == 0 else z
        value = part_ref[core, at, zz, h].astype(jnp.float32) + mate[at, zz, h].astype(jnp.float32)
        if (zi, h) == (1, 3):
            crosses[dy].wait_recv()
            value = value + zin[dy].astype(jnp.float32)
        return value

    crosses = {}

    def cross(n, value):
        zout[n] = value.astype(jnp.bfloat16)
        crosses[n] = pltpu.make_async_remote_copy(
            src_ref=zout.at[n],
            dst_ref=zin.at[n],
            send_sem=z_send.at[n],
            recv_sem=z_recv.at[n],
            device_id={"rep": across},
            device_id_type=MESH,
        )
        crosses[n].start()

    def hops(d, h):
        return 4 if d != h // 2 else 3

    copies = {}
    for s in range(4):
        for zi in range(2):
            if (s, zi) == (0, 1):
                for dy in (4, 5, 3, 6, 2, 7, 1, 0):
                    cross(dy, term(dy, 0, 3))
            for d, h in ((0, 2), (1, 0), (1, 1), (0, 0), (1, 2), (0, 1), (0, 3), (1, 3)):
                length = hops(d, h)
                if s >= length or (zi, h) == (0, 3):
                    continue
                dy = (length - s) * (1 - 2 * d)
                value = term(dy, zi, h)
                if s == 0:
                    buf = first.at[d, h, zi]
                else:
                    copies[d, h, zi, s - 1].wait_recv()
                    buf = runs.at[d, h, zi, s - 1]
                    value = value + buf[...].astype(jnp.float32)
                buf[...] = value.astype(jnp.bfloat16)
                copies[d, h, zi, s] = pltpu.make_async_remote_copy(
                    src_ref=buf,
                    dst_ref=runs.at[d, h, zi, s],
                    send_sem=run_send.at[d, h, zi, s],
                    recv_sem=run_recv.at[d, h, zi, s],
                    device_id={"rep": steps[d]},
                    device_id_type=MESH,
                )
                copies[d, h, zi, s].start()

    def gathered(zi, h):
        value = term(0, zi, h)
        for d in range(2):
            last = hops(d, h) - 1
            copies[d, h, zi, last].wait_recv()
            value = value + runs[d, h, zi, last].astype(jnp.float32)
        return value

    for h in range(3):
        cross(8 + h, gathered(0, h))
    mine = [gathered(1, h) for h in range(4)]
    out_ref[3 * part :, :] = mine[3]
    for h in range(3):
        crosses[8 + h].wait_recv()
        out_ref[h * part : (h + 1) * part, :] = mine[h] + zin[8 + h].astype(jnp.float32)
    for copy in list(swaps.values()) + list(copies.values()) + list(crosses.values()):
        copy.wait_send()


def shards(
    features, inv_degree, weight, bias_vector, tile_values, tile_rows, tile_cols, tile_counts
):
    rows_dev, width = features.shape
    sections, caps, tile = tile_values.shape[1:4]
    vmem = pl.BlockSpec(memory_space=pltpu.VMEM)
    hbm = pl.BlockSpec(memory_space=pltpu.HBM)
    bf16, f32 = jnp.bfloat16, jnp.float32
    dma = pltpu.SemaphoreType.DMA
    products = pl.pallas_call(
        gather_kernel,
        out_shape=pltpu.VMEM((sections, 2, caps, tile, width), f32),
        in_specs=[hbm, hbm, hbm],
        out_specs=vmem,
        scratch_shapes=[
            pltpu.VMEM((sections, rows_dev, width), bf16),
            pltpu.VMEM(tile_values.shape[1:], bf16),
            pltpu.VMEM((rows_dev, width), bf16),
            pltpu.VMEM((2, rows_dev // 2), f32),
            dma((60,)),
            dma((16, 4)),
            dma((2,)),
            dma((sections,)),
        ],
        compiler_params=pltpu.CompilerParams(
            collective_id=0, has_side_effects=True, vmem_limit_bytes=46 * MIB
        ),
        cost_estimate=pl.CostEstimate(flops=0, bytes_accessed=48 * MIB, transcendentals=0),
        name="gather_pieces",
    )(features, inv_degree.reshape(2, rows_dev // 2), tile_values[0])
    partial = pl.pallas_call(
        tiles_kernel,
        out_shape=jax.ShapeDtypeStruct((2, 8, 2, 4, tile // 2, width), bf16),
        in_specs=[hbm, hbm, hbm, vmem],
        out_specs=vmem,
        scratch_shapes=[
            pltpu.SMEM((caps, sections), jnp.int32),
            pltpu.SMEM((caps, sections), jnp.int32),
            pltpu.SMEM((1, sections), jnp.int32),
            pltpu.VMEM((65, tile, width), f32),
            dma((3,)),
        ],
        compiler_params=pltpu.CompilerParams(vmem_limit_bytes=20 * MIB),
        name="tile_products",
    )(tile_rows[0].T, tile_cols[0].T, tile_counts, products)
    summed = pl.pallas_call(
        scatter_kernel,
        out_shape=jax.ShapeDtypeStruct((rows_dev, width), f32),
        in_specs=[vmem],
        out_specs=vmem,
        scratch_shapes=[
            pltpu.VMEM((8, 2, 4, tile // 2, width), bf16),
            pltpu.VMEM((2, 4, 2, tile // 2, width), bf16),
            pltpu.VMEM((2, 4, 2, 4, tile // 2, width), bf16),
            pltpu.VMEM((11, tile // 2, width), bf16),
            pltpu.VMEM((11, tile // 2, width), bf16),
            dma((8,)),
            dma((8,)),
            dma((2, 4, 2, 4)),
            dma((2, 4, 2, 4)),
            dma((11,)),
            dma((11,)),
        ],
        compiler_params=pltpu.CompilerParams(
            collective_id=1, has_side_effects=True, vmem_limit_bytes=16 * MIB
        ),
        cost_estimate=pl.CostEstimate(flops=0, bytes_accessed=48 * MIB, transcendentals=0),
        name="scatter_sums",
    )(partial)
    normed = (inv_degree[:, None] * summed).astype(bf16)
    hidden = jnp.dot(normed, weight, preferred_element_type=f32) + bias_vector
    return jnp.maximum(hidden, 0.0).astype(bf16)


def solution(mesh):
    return jax.shard_map(
        shards,
        mesh=mesh,
        in_specs=(
            P(("section", "rep"), None),
            P(("section", "rep")),
            P(),
            P(),
            P(("section", "rep"), None, None, None, None),
            P(("section", "rep"), None, None),
            P(("section", "rep"), None, None),
            P(("section", "rep"), None),
        ),
        out_specs=P(("section", "rep"), None),
        check_vma=False,
    )
```
